32 devices in a mesh: wave: 16 (over z, x, core), rows: 2 (over y).
Axes of the slice: x: 2, y: 2, z: 4, core: 2. Of those that a mesh axis runs over, the one named last changes fastest.
Arguments:
- potential: bfloat16 [4, 128, 2048], P(None, 'rows', 'wave'), may hold values from 0 to 1
- tilt_index: int32 [32, 2], P('wave'), may hold values from -128 to 127
Outputs:
- exit_wave: bfloat16 [2, 32, 128, 2048], P(None, 'wave', 'rows')
The draws below stay inside these ranges and needn't reach their ends.
All inputs are finite; a program needn't handle non-finite values.
Results may differ from the reference program's by a relative error of at most 0.025.
Values may be sent and summed in bfloat16 or wider, within the bound.
A program may use at most 64 MiB of HBM per device.

```python
import math
import jax
import jax.numpy as jnp
from jax import lax

NX = 2048
TAPS = 33
BLOCK = 128
SLICES = 4
ROWS_DEV = 64
NY = 128
WAVES = 32


def touch_ends(drawn, rng, low, top_value):
    longest = drawn.shape.index(max(drawn.shape))
    spots = []
    for shift in (0, 1):
        where = [jax.random.randint(jax.random.fold_in(rng, axis), (), 0, length) for axis, length in enumerate(drawn.shape)]
        where[longest] = (where[longest] + shift) % drawn.shape[longest]
        spots.append(tuple(where))
    return drawn.at[spots[0]].set(low).at[spots[1]].set(top_value)


def level_of(key, shape, split, smallest, top_value):
    factor_of, own = 1.0, jax.random.fold_in(key, 6)
    for position, blocks in split:
        heights = jnp.exp(jax.random.uniform(jax.random.fold_in(own, position), (blocks,), jnp.float32, smallest / len(split), top_value / len(split)))
        factor_of = factor_of * jnp.repeat(heights, shape[position] // blocks).reshape([-1 if axis == position else 1 for axis in range(len(shape))])
    return factor_of


def setup_inputs(seed: int = 0) -> dict:
    arg_keys = jax.random.split(jax.random.key(seed), 3)
    potential = jnp.clip(1.0 * jax.random.uniform(arg_keys[0], (SLICES, NY, NX), jnp.float32) ** level_of(arg_keys[0], (SLICES, NY, NX), ((1, 2), (2, 16)), -0.2, 0.2), 0.0, 1.0).astype(jnp.bfloat16)
    tilt_index = touch_ends(jax.random.randint(arg_keys[1], (WAVES, 2), -128, 128), jax.random.fold_in(arg_keys[1], 1), -128, 127).astype(jnp.int32)
    return dict(potential=potential, tilt_index=tilt_index)


def band_kernel(width):
    reach = TAPS // 2
    inner = jnp.arange(width + 2 * reach)[:, None]
    outer = jnp.arange(width)[None, :]
    offset = inner - outer
    valid = (offset >= 0) & (offset < TAPS)
    centred = (offset - reach).astype(jnp.float32)
    angle_val = math.pi * centred * centred / TAPS
    weight = jnp.where(valid, 1.0 / math.sqrt(TAPS), 0.0).astype(jnp.float32)
    real_part = (jnp.cos(angle_val) * weight).astype(jnp.bfloat16)
    imag_part = (jnp.sin(angle_val) * weight).astype(jnp.bfloat16)
    return jnp.stack([jnp.stack([real_part, imag_part]), jnp.stack([-imag_part, real_part])])

def column_pass(field, kernel):
    reach = TAPS // 2
    padded = jnp.pad(field, ((0, 0), (0, 0), (reach, reach)))
    count = field.shape[2] // BLOCK
    windows = jnp.stack([padded[:, :, b * BLOCK:b * BLOCK + BLOCK + 2 * reach] for b in range(count)], axis=2)
    result = jnp.einsum('prbm,pqmc->qrbc', windows.astype(jnp.float32), kernel.astype(jnp.float32))
    return result.reshape(field.shape)

def row_pass(padded, kernel, row_block):
    reach = TAPS // 2
    total = padded.shape[1] - 2 * reach
    count = total // row_block
    windows = jnp.stack([padded[:, b * row_block:b * row_block + row_block + 2 * reach, :] for b in range(count)], axis=1)
    result = jnp.einsum('pbmc,pqmr->qbrc', windows.astype(jnp.float32), kernel.astype(jnp.float32))
    return result.reshape((2, total, padded.shape[2]))

def reference(potential, tilt_index):
    reach = TAPS // 2
    row_block = min(BLOCK, ROWS_DEV)
    col_kernel = band_kernel(BLOCK)
    row_kernel = band_kernel(row_block)
    phase_val = 3.0 * potential.astype(jnp.float32)
    trans_re = jnp.cos(phase_val).astype(jnp.bfloat16)
    trans_im = jnp.sin(phase_val).astype(jnp.bfloat16)
    y_index = jnp.arange(NY, dtype=jnp.int32)
    x_index = jnp.arange(NX, dtype=jnp.int32)

    def one_wave(tilt):
        y_turn = (tilt[0] * y_index % NY).astype(jnp.float32) / NY
        x_turn = (tilt[1] * x_index % NX).astype(jnp.float32) / NX
        angle_val = 2.0 * math.pi * (y_turn[:, None] + x_turn[None, :])
        wave = jnp.stack([jnp.cos(angle_val), jnp.sin(angle_val)]).astype(jnp.bfloat16)
        for slice_num in range(SLICES):
            wave_re = wave[0].astype(jnp.float32)
            wave_im = wave[1].astype(jnp.float32)
            t_re = trans_re[slice_num].astype(jnp.float32)
            t_im = trans_im[slice_num].astype(jnp.float32)
            moved = jnp.stack([wave_re * t_re - wave_im * t_im, wave_re * t_im + wave_im * t_re]).astype(jnp.bfloat16)
            half_step = column_pass(moved, col_kernel).astype(jnp.bfloat16)
            padded = jnp.pad(half_step, ((0, 0), (reach, reach), (0, 0)))
            wave = row_pass(padded, row_kernel, row_block).astype(jnp.bfloat16)
        return wave
    waves_out = lax.map(one_wave, tilt_index)
    return jnp.transpose(waves_out, (1, 0, 2, 3))
```

```python
import functools
import math

import jax
import jax.numpy as jnp
import numpy as np
from jax import lax
from jax.experimental import pallas as pl
from jax.experimental.pallas import tpu as pltpu
from jax.sharding import PartitionSpec as P

TAPS = 33
REACH = TAPS // 2
LANES = 128
GROUP = 4
MESH = pl.DeviceIdType.MESH

SIN_COEF = (9.99999997e-01, -1.66666606e-01, 8.33311822e-03, -1.98143924e-04, 2.61811836e-06)
COS_COEF = (9.99999970e-01, -4.99999341e-01, 4.16643157e-02, -1.38594940e-03, 2.32943501e-05)


def tap_parts(offset):
    centred = (offset - REACH).astype(jnp.float32)
    angle_val = math.pi * centred * centred / TAPS
    valid = (offset >= 0) & (offset < TAPS)
    weight = jnp.where(valid, 1.0 / math.sqrt(TAPS), 0.0).astype(jnp.float32)
    real_part = (jnp.cos(angle_val) * weight).astype(jnp.bfloat16)
    imag_part = (jnp.sin(angle_val) * weight).astype(jnp.bfloat16)
    return real_part, imag_part


def tile_band():
    inner = jnp.arange(LANES)[:, None]
    outer = jnp.arange(LANES)[None, :]
    beside = jnp.where(inner < LANES // 2, inner + LANES, inner - LANES)
    parts = []
    for source in (inner, beside):
        real_part, imag_part = tap_parts(source - outer + REACH)
        top = jnp.concatenate([real_part, imag_part], axis=1)
        low = jnp.concatenate([-imag_part, real_part], axis=1)
        parts.append(jnp.concatenate([top, low], axis=0))
    return jnp.stack(parts)


class Plan:
    def __init__(self, slices, rows_local, count):
        self.sides = min(count - 1, 2)
        self.rows_local, self.count, self.slices = rows_local, count, slices
        self.high = [rows_local + self.sides * REACH * (slices - s) for s in range(slices + 1)]
        self.stored = rows_local * (1 + self.sides)

    def start(self, s, r):
        if self.sides == 0:
            return 0 * r
        if self.sides == 1:
            return r * (2 * self.rows_local - self.high[s])
        return r * self.rows_local - REACH * (self.slices - s)

    def stored_offset(self, s, r):
        if self.sides == 2:
            return self.rows_local - REACH * (self.slices - s)
        return self.start(s, r)

    def row_matrix(self, s, r):
        out_row = jnp.arange(self.high[s + 1])[:, None] + self.start(s + 1, r)
        in_row = jnp.arange(self.high[s])[None, :] + self.start(s, r)
        inside = (in_row >= 0) & (in_row < self.rows_local * self.count)
        real_part, imag_part = tap_parts(jnp.where(inside, in_row - out_row + REACH, -1))
        top = jnp.concatenate([real_part, -imag_part], axis=1)
        low = jnp.concatenate([imag_part, real_part], axis=1)
        return jnp.concatenate([top, low], axis=0)


def horner(square, coefs):
    total = square * coefs[-1] + coefs[-2]
    for coef in coefs[-3::-1]:
        total = total * square + coef
    return total


def transmission(pot):
    turn = 3.0 * pot.astype(jnp.float32) - 1.5
    square = turn * turn
    sine = horner(square, SIN_COEF) * turn
    cosine = horner(square, COS_COEF)
    mid_cos, mid_sin = math.cos(1.5), math.sin(1.5)
    return cosine * mid_cos - sine * mid_sin, sine * mid_cos + cosine * mid_sin


def modulo(value, size):
    if size & (size - 1) == 0:
        return value & (size - 1)
    return lax.rem(lax.rem(value, size) + size, size)


def gather_steps(plan, column_groups, shard, full, sems):
    send1, recv1, send2, recv2, send3, recv3, own = sems
    me, r = lax.axis_index("wave"), lax.axis_index("rows")
    z, q = me // GROUP, me % GROUP
    x, c = q // 2, q % 2
    rows = plan.rows_local
    flip_x = z * GROUP + (1 - x) * 2 + c
    sibling = z * GROUP + x * 2 + (1 - c)

    def block(s, column, row_dev, trimmed):
        need = REACH * (plan.slices - s) if trimmed else rows
        start = row_dev * rows + (1 - row_dev) * (rows - need)
        return full.at[s, :, column, pl.ds(pl.multiple_of(start, REACH), need), :]

    def remote(src, dst, send, recv, wave, row):
        return pltpu.make_async_remote_copy(
            src_ref=src, dst_ref=dst, send_sem=send, recv_sem=recv, device_id=(wave, row), device_id_type=MESH
        )

    barrier = pltpu.get_barrier_semaphore()
    others = [((z + d) % column_groups * GROUP + q, r) for d in range(1, column_groups)]
    peers = others + [(flip_x, r), (me, 1 - r), (flip_x, 1 - r), (sibling, r)]
    for peer in peers:
        pl.semaphore_signal(barrier, inc=1, device_id=peer, device_id_type=MESH)
    pl.semaphore_wait(barrier, len(peers))

    first, second, third, local = [], [], [], []
    for s in range(plan.slices):
        place = full.at[s, z, q, pl.ds(pl.multiple_of(r * rows, rows), rows), :]
        local.append(pltpu.make_async_copy(shard.at[s], place, own.at[s]))
        first.append([
            remote(shard.at[s], place, send1.at[s, d], recv1.at[s, d], *others[d])
            for d in range(column_groups - 1)
        ])
        mine, mine_cut = block(s, q, r, False), block(s, q, r, True)
        second.append([
            remote(mine, mine, send2.at[s, 0], recv2.at[s, 0], flip_x, r),
            remote(mine_cut, mine_cut, send2.at[s, 1], recv2.at[s, 1], me, 1 - r),
            remote(mine_cut, mine_cut, send2.at[s, 2], recv2.at[s, 2], flip_x, 1 - r),
        ])
        held = [
            mine,
            block(s, (1 - x) * 2 + c, r, False),
            block(s, q, 1 - r, True),
            block(s, (1 - x) * 2 + c, 1 - r, True),
        ]
        third.append([
            remote(held[k], held[k], send3.at[s, k], recv3.at[s, k], sibling, r) for k in range(4)
        ])
    return local, first, second, third


def device_kernel(plan, waves, gather, tilt, shard, band, *rest):
    slices = plan.slices
    row_mats, out = rest[:slices], rest[slices]
    scratch = rest[slices + 1 :]
    r = lax.axis_index("rows")
    if gather:
        full, moved, col_turn, row_turn = scratch[:4]
    else:
        full = shard
        moved, col_turn, row_turn = scratch[:3]
    column_groups = full.shape[1]
    tiles = column_groups * GROUP
    plane_rows = plan.rows_local * plan.count

    if gather:
        local, first, second, third = gather_steps(plan, column_groups, shard, full, scratch[4:])
        for s in range(slices):
            for copy in first[s]:
                copy.start()
            local[s].start()

    def relay_columns(s):
        if gather:
            for copy in first[s]:
                copy.wait_recv()
            local[s].wait()
            for copy in second[s]:
                copy.start()
            third[s][0].start()

    def relay_sibling(s):
        if gather:
            for k in range(3):
                second[s][k].wait_recv()
                third[s][k + 1].start()

    def arrive(s):
        if gather:
            for copy in third[s]:
                copy.wait_recv()

    for b in range(waves):
        column = lax.broadcasted_iota(jnp.int32, (tiles, LANES), 0) * LANES
        column = column + lax.broadcasted_iota(jnp.int32, (tiles, LANES), 1)
        size = tiles * LANES
        turn = modulo(tilt[b, 1] * column, size).astype(jnp.float32) * (2.0 * math.pi / size)
        col_turn[b, 0] = jnp.cos(turn)
        col_turn[b, 1] = jnp.sin(turn)
        row = lax.broadcasted_iota(jnp.int32, (plan.high[0], LANES), 0) + plan.start(0, r)
        turn = modulo(tilt[b, 0] * row, plane_rows).astype(jnp.float32) * (2.0 * math.pi / plane_rows)
        row_turn[b, 0] = jnp.cos(turn)
        row_turn[b, 1] = jnp.sin(turn)
    for half in range(2):
        for edge in (0, tiles + 1):
            moved[half, edge] = jnp.zeros(moved.shape[2:], moved.dtype)

    def transmit(s, group, lane, source):
        high = plan.high[s]
        offset = plan.stored_offset(s, r)
        for k in range(high // REACH):
            at = offset + k * REACH
            if not isinstance(at, int):
                at = pl.multiple_of(at, REACH)
            t_re, t_im = transmission(full[s, group, lane, pl.ds(at, REACH), :])
            for b in range(waves):
                w_re, w_im = source(k, b)
                to = moved.at[s % 2, group * GROUP + lane + 1, pl.ds(b * high + k * REACH, REACH)]
                to[:, :LANES] = (w_re * t_re - w_im * t_im).astype(jnp.bfloat16)
                to[:, LANES:] = (w_re * t_im + w_im * t_re).astype(jnp.bfloat16)

    for s in range(slices):
        relay_columns(s)
    relay_sibling(0)
    arrive(0)

    def begin(group, carry):
        for lane in range(GROUP):
            tile = group * GROUP + lane

            def source(k, b):
                c_re, c_im = col_turn[b, 0, pl.ds(tile, 1), :], col_turn[b, 1, pl.ds(tile, 1), :]
                span = pl.ds(k * REACH, REACH)
                r_re, r_im = row_turn[b, 0, span, :], row_turn[b, 1, span, :]
                return r_re * c_re - r_im * c_im, r_re * c_im + r_im * c_re

            transmit(0, group, lane, source)
        return carry

    lax.fori_loop(0, column_groups, begin, 0)

    for s in range(slices):
        high, low = plan.high[s], plan.high[s + 1]
        if s + 1 < slices:
            relay_sibling(s + 1)
            arrive(s + 1)

        def advance(group, carry):
            which = lax.broadcasted_iota(jnp.int32, (waves * high, 2 * LANES), 1) % LANES < LANES // 2
            for lane in range(GROUP):
                tile = group * GROUP + lane
                span = pl.ds(0, waves * high)
                beside = jnp.where(which, moved[s % 2, tile + 2, span], moved[s % 2, tile, span])
                half_step = jnp.dot(moved[s % 2, tile + 1, span], band[0], preferred_element_type=jnp.float32)
                half_step += jnp.dot(beside, band[1], preferred_element_type=jnp.float32)
                half_step = half_step.astype(jnp.bfloat16)
                stacked = jnp.concatenate(
                    [
                        jnp.concatenate(
                            [half_step[b * high : (b + 1) * high, p * LANES : (p + 1) * LANES] for b in range(waves)],
                            axis=1,
                        )
                        for p in range(2)
                    ],
                    axis=0,
                )
                result = jnp.dot(row_mats[s][...], stacked, preferred_element_type=jnp.float32)
                if s + 1 < slices:

                    def source(k, b):
                        span_b = slice(b * LANES, (b + 1) * LANES)
                        at = k * REACH
                        return result[at : at + REACH, span_b], result[low + at : low + at + REACH, span_b]

                    transmit(s + 1, group, lane, source)
                else:
                    columns = pl.ds(pl.multiple_of(tile * LANES, LANES), LANES)
                    for p in range(2):
                        for b in range(waves):
                            part = result[p * low : (p + 1) * low, b * LANES : (b + 1) * LANES]
                            out[p, b, :, columns] = part.astype(jnp.bfloat16)
            return carry

        lax.fori_loop(0, column_groups, advance, 0)

    if gather:
        for s in range(slices):
            for copy in first[s] + second[s] + third[s]:
                copy.wait_send()


def per_device(potential, tilt_index):
    slices, rows_local, width = potential.shape
    waves = tilt_index.shape[0]
    across, count = lax.axis_size("wave"), lax.axis_size("rows")
    plan = Plan(slices, rows_local, count)
    r = lax.axis_index("rows")
    tiles = width * across // LANES
    gather = count == 2 and width == LANES and across % GROUP == 0
    source = potential
    if not gather:
        plane = lax.all_gather(potential, "wave", axis=2, tiled=True)
        if plan.sides:
            up = [(i, i + 1) for i in range(count - 1)]
            above = lax.ppermute(plane, "rows", up)
            below = lax.ppermute(plane, "rows", [(b, a) for a, b in up])
            if plan.sides == 2:
                plane = jnp.concatenate([above, plane, below], axis=1)
            else:
                plane = jnp.concatenate(
                    [jnp.where(r == 0, plane, above), jnp.where(r == 0, below, plane)], axis=1
                )
        plane = plane.reshape(slices, plan.stored, tiles // GROUP, GROUP, LANES)
        source = plane.transpose(0, 2, 3, 1, 4)
    row_mats = [plan.row_matrix(s, r) for s in range(slices)]
    vmem = pl.BlockSpec(memory_space=pltpu.VMEM)
    scratch = [
        pltpu.VMEM((2, tiles + 2, waves * plan.high[0], 2 * LANES), jnp.bfloat16),
        pltpu.VMEM((waves, 2, tiles, LANES), jnp.float32),
        pltpu.VMEM((waves, 2, plan.high[0], LANES), jnp.float32),
    ]
    params = {}
    if gather:
        groups = across // GROUP
        scratch = [pltpu.VMEM((slices, groups, GROUP, plan.stored, LANES), jnp.bfloat16)] + scratch
        for size in (groups - 1, groups - 1, 3, 3, 4, 4):
            scratch.append(pltpu.SemaphoreType.DMA((slices, size)))
        scratch.append(pltpu.SemaphoreType.DMA((slices,)))
        params = dict(collective_id=0, has_side_effects=True)
    return pl.pallas_call(
        functools.partial(device_kernel, plan, waves, gather),
        out_shape=jax.ShapeDtypeStruct((2, waves, rows_local, width * across), jnp.bfloat16),
        in_specs=[pl.BlockSpec(memory_space=pltpu.SMEM)] + [vmem] * (2 + slices),
        out_specs=vmem,
        scratch_shapes=scratch,
        compiler_params=pltpu.CompilerParams(vmem_limit_bytes=60 * 1024 * 1024, **params),
    )(tilt_index, source, tile_band(), *row_mats)


def solution(mesh):
    placed = (P(None, "rows", "wave"), P("wave", None))
    return jax.shard_map(
        per_device,
        mesh=mesh,
        in_specs=placed,
        out_specs=P(None, "wave", "rows", None),
        check_vma=False,
    )
```

```python
import functools
import math

import jax
import jax.numpy as jnp
import numpy as np
from jax import lax
from jax.experimental import pallas as pl
from jax.experimental.pallas import tpu as pltpu
from jax.sharding import PartitionSpec as P

TAPS = 33
REACH = TAPS // 2
LANES = 128
GROUP = 4
MESH = pl.DeviceIdType.MESH

MIDDLE = 1.5
SIN_COEF = (9.99999997e-01, -1.66666606e-01, 8.33311822e-03, -1.98143924e-04, 2.61811836e-06)
COS_COEF = (9.99999970e-01, -4.99999341e-01, 4.16643157e-02, -1.38594940e-03, 2.32943501e-05)


def tap_parts(offset, np=np):
    centred = (offset - REACH).astype(np.float32)
    angle_val = np.float32(math.pi) * centred * centred / np.float32(TAPS)
    valid = (offset >= 0) & (offset < TAPS)
    weight = np.where(valid, 1.0 / math.sqrt(TAPS), 0.0).astype(np.float32)
    real_part = (np.cos(angle_val) * weight).astype(jnp.bfloat16)
    imag_part = (np.sin(angle_val) * weight).astype(jnp.bfloat16)
    return real_part, imag_part


def tile_band():
    inner = np.arange(LANES)[:, None]
    outer = np.arange(LANES)[None, :]
    beside = np.where(inner < LANES // 2, inner + LANES, inner - LANES)
    parts = []
    for source in (inner, beside):
        real_part, imag_part = tap_parts(source - outer + REACH)
        top = np.concatenate([real_part, imag_part], axis=1)
        low = np.concatenate([-imag_part, real_part], axis=1)
        parts.append(np.concatenate([top, low], axis=0))
    return np.concatenate(parts, axis=0)


class Plan:
    def __init__(self, slices, rows_local, count):
        self.sides = min(count - 1, 2)
        self.rows_local, self.count, self.slices = rows_local, count, slices
        self.high = [rows_local + self.sides * REACH * (slices - s) for s in range(slices + 1)]
        self.stored = rows_local * (1 + self.sides)

    def start(self, s, r):
        if self.sides == 0:
            return 0 * r
        if self.sides == 1:
            return r * (2 * self.rows_local - self.high[s])
        return r * self.rows_local - REACH * (self.slices - s)

    def stored_offset(self, s, r):
        if self.sides == 2:
            return self.rows_local - REACH * (self.slices - s)
        return self.start(s, r)

    def row_matrix(self, s, r, np=np):
        out_row = np.arange(self.high[s + 1])[:, None] + self.start(s + 1, r)
        in_row = np.arange(self.high[s])[None, :] + self.start(s, r)
        inside = (in_row >= 0) & (in_row < self.rows_local * self.count)
        real_part, imag_part = tap_parts(np.where(inside, in_row - out_row + REACH, -1), np)
        top = np.concatenate([real_part, -imag_part], axis=1)
        low = np.concatenate([imag_part, real_part], axis=1)
        return np.concatenate([top, low], axis=0)


def horner(square, coefs):
    total = square * coefs[-1] + coefs[-2]
    for coef in coefs[-3::-1]:
        total = total * square + coef
    return total


def transmission(pot):
    turn = 3.0 * pot.astype(jnp.float32) - MIDDLE
    square = turn * turn
    return horner(square, COS_COEF), horner(square, SIN_COEF) * turn


def modulo(value, size):
    if size & (size - 1) == 0:
        return value & (size - 1)
    return lax.rem(lax.rem(value, size) + size, size)


def gather_steps(plan, column_groups, shard, full, sems):
    send1, recv1, send2, recv2, send3, recv3, own = sems
    me, r = lax.axis_index("wave"), lax.axis_index("rows")
    z, q = me // GROUP, me % GROUP
    x, c = q // 2, q % 2
    rows = plan.rows_local
    flip_x = z * GROUP + (1 - x) * 2 + c
    sibling = z * GROUP + x * 2 + (1 - c)

    def block(s, column, row_dev, trimmed):
        need = REACH * (plan.slices - s) if trimmed else rows
        start = row_dev * rows + (1 - row_dev) * (rows - need)
        return full.at[s, :, column, pl.ds(pl.multiple_of(start, REACH), need), :]

    def remote(src, dst, send, recv, wave, row):
        return pltpu.make_async_remote_copy(
            src_ref=src, dst_ref=dst, send_sem=send, recv_sem=recv, device_id=(wave, row), device_id_type=MESH
        )

    barrier = pltpu.get_barrier_semaphore()
    others = [((z + d) % column_groups * GROUP + q, r) for d in range(1, column_groups)]
    peers = others + [(flip_x, r), (me, 1 - r), (flip_x, 1 - r), (sibling, r)]
    for peer in peers:
        pl.semaphore_signal(barrier, inc=1, device_id=peer, device_id_type=MESH)
    pl.semaphore_wait(barrier, len(peers))

    first, second, third, local = [], [], [], []
    for s in range(plan.slices):
        place = full.at[s, z, q, pl.ds(pl.multiple_of(r * rows, rows), rows), :]
        local.append(pltpu.make_async_copy(shard.at[s], place, own.at[s]))
        first.append([
            remote(shard.at[s], place, send1.at[s, d], recv1.at[s, d], *others[d])
            for d in range(column_groups - 1)
        ])
        mine, mine_cut = block(s, q, r, False), block(s, q, r, True)
        second.append([
            remote(mine, mine, send2.at[s, 0], recv2.at[s, 0], flip_x, r),
            remote(mine_cut, mine_cut, send2.at[s, 1], recv2.at[s, 1], me, 1 - r),
            remote(mine_cut, mine_cut, send2.at[s, 2], recv2.at[s, 2], flip_x, 1 - r),
        ])
        held = [
            mine,
            block(s, (1 - x) * 2 + c, r, False),
            block(s, q, 1 - r, True),
            block(s, (1 - x) * 2 + c, 1 - r, True),
        ]
        third.append([
            remote(held[k], held[k], send3.at[s, k], recv3.at[s, k], sibling, r) for k in range(4)
        ])
    return local, first, second, third


def device_kernel(plan, waves, gather, tilt, shard, band, *rest):
    slices = plan.slices
    row_mats, out = rest[:slices], rest[slices]
    scratch = rest[slices + 1 :]
    r = lax.axis_index("rows")
    if gather:
        full, moved, halves, col_turn, row_turn = scratch[:5]
    else:
        full = shard
        moved, halves, col_turn, row_turn = scratch[:4]
    column_groups = full.shape[1]
    tiles = column_groups * GROUP
    plane_rows = plan.rows_local * plan.count

    if gather:
        local, first, second, third = gather_steps(plan, column_groups, shard, full, scratch[5:])
        for s in range(slices):
            local[s].start()
        for copy in first[0]:
            copy.start()

    def relay_columns(s):
        if gather:
            for copy in first[s]:
                copy.wait_recv()
            local[s].wait()
            for copy in second[s]:
                copy.start()
            third[s][0].start()
            for copy in first[s + 1] if s + 1 < slices else []:
                copy.start()

    def relay_sibling(s):
        if gather:
            for k in range(3):
                second[s][k].wait_recv()
                third[s][k + 1].start()

    def arrive(s):
        if gather:
            for copy in third[s]:
                copy.wait_recv()

    for b in range(waves):
        column = lax.broadcasted_iota(jnp.int32, (tiles, LANES), 0) * LANES
        column = column + lax.broadcasted_iota(jnp.int32, (tiles, LANES), 1)
        size = tiles * LANES
        turn = modulo(tilt[b, 1] * column, size).astype(jnp.float32) * (2.0 * math.pi / size)
        col_turn[b, 0] = jnp.cos(turn)
        col_turn[b, 1] = jnp.sin(turn)
        row = lax.broadcasted_iota(jnp.int32, (plan.high[0], LANES), 0) + plan.start(0, r)
        turn = modulo(tilt[b, 0] * row, plane_rows).astype(jnp.float32) * (2.0 * math.pi / plane_rows)
        turn = turn + slices * MIDDLE
        row_turn[b, 0] = jnp.cos(turn)
        row_turn[b, 1] = jnp.sin(turn)
    for half in range(2):
        for edge in (0, tiles + 1):
            moved[half, edge] = jnp.zeros(moved.shape[2:], moved.dtype)

    def transmit(s, group, lane, source):
        high = plan.high[s]
        offset = plan.stored_offset(s, r)
        for k in range(high // REACH):
            at = offset + k * REACH
            if not isinstance(at, int):
                at = pl.multiple_of(at, REACH)
            t_re, t_im = transmission(full[s, group, lane, pl.ds(at, REACH), :])
            for b in range(waves):
                w_re, w_im = source(k, b)
                to = moved.at[s % 2, group * GROUP + lane + 1, pl.ds(b * high + k * REACH, REACH)]
                to[:, :LANES] = (w_re * t_re - w_im * t_im).astype(jnp.bfloat16)
                to[:, LANES:] = (w_re * t_im + w_im * t_re).astype(jnp.bfloat16)

    relay_columns(0)
    relay_sibling(0)
    relay_columns(1)
    arrive(0)

    def begin(group, carry):
        for lane in range(GROUP):
            tile = group * GROUP + lane

            def source(k, b):
                c_re, c_im = col_turn[b, 0, pl.ds(tile, 1), :], col_turn[b, 1, pl.ds(tile, 1), :]
                span = pl.ds(k * REACH, REACH)
                r_re, r_im = row_turn[b, 0, span, :], row_turn[b, 1, span, :]
                return r_re * c_re - r_im * c_im, r_re * c_im + r_im * c_re

            transmit(0, group, lane, source)
        return carry

    lax.fori_loop(0, column_groups, begin, 0)

    def column_pass(s, group):
        rows = waves * plan.high[s]
        tile = group * GROUP

        def tiles_from(first_tile):
            return moved[s % 2, pl.ds(first_tile, GROUP), pl.ds(0, rows)].reshape(GROUP * rows, 2 * LANES)

        lane = lax.broadcasted_iota(jnp.int32, (GROUP * rows, 2 * LANES), 1) % LANES
        beside = jnp.where(lane < LANES // 2, tiles_from(tile + 2), tiles_from(tile))
        window = jnp.concatenate([tiles_from(tile + 1), beside], axis=1)
        half_step = jnp.dot(window, band[...], preferred_element_type=jnp.float32).astype(jnp.bfloat16)
        halves[group % 2, :, pl.ds(0, rows)] = half_step.reshape(GROUP, rows, 2 * LANES)

    def row_pass(s, group):
        high, low = plan.high[s], plan.high[s + 1]
        matrix = row_mats[s][r if plan.count <= 2 else 0]
        for lane in range(GROUP):
            stacked = jnp.concatenate(
                [
                    jnp.concatenate(
                        [
                            halves[group % 2, lane, pl.ds(b * high, high), pl.ds(p * LANES, LANES)]
                            for b in range(waves)
                        ],
                        axis=1,
                    )
                    for p in range(2)
                ],
                axis=0,
            )
            result = jnp.dot(matrix, stacked, preferred_element_type=jnp.float32)
            if s + 1 < slices:

                def source(k, b):
                    span_b = slice(b * LANES, (b + 1) * LANES)
                    at = k * REACH
                    return result[at : at + REACH, span_b], result[low + at : low + at + REACH, span_b]

                transmit(s + 1, group, lane, source)
            else:
                start = (group * GROUP + lane) * LANES
                columns = pl.ds(start if isinstance(start, int) else pl.multiple_of(start, LANES), LANES)
                for p in range(2):
                    for b in range(waves):
                        part = result[p * low : (p + 1) * low, b * LANES : (b + 1) * LANES]
                        out[p, b, :, columns] = part.astype(jnp.bfloat16)

    last = column_groups - 1
    relay_sibling(1)
    relay_columns(2)
    arrive(1)
    column_pass(0, 0)
    for s in range(slices):

        def advance(group, carry):
            column_pass(s, group + 1)
            row_pass(s, group)
            return carry

        lax.fori_loop(0, last, advance, 0)
        row_pass(s, last)
        if s + 1 < slices:
            column_pass(s + 1, 0)
        if s + 2 < slices:
            relay_sibling(s + 2)
            if s + 3 < slices:
                relay_columns(s + 3)
            arrive(s + 2)

    if gather:
        for s in range(slices):
            for copy in first[s] + second[s] + third[s]:
                copy.wait_send()


def per_device(potential, tilt_index):
    slices, rows_local, width = potential.shape
    waves = tilt_index.shape[0]
    across, count = lax.axis_size("wave"), lax.axis_size("rows")
    plan = Plan(slices, rows_local, count)
    r = lax.axis_index("rows")
    tiles = width * across // LANES
    gather = count == 2 and width == LANES and across % GROUP == 0
    source = potential
    if not gather:
        plane = lax.all_gather(potential, "wave", axis=2, tiled=True)
        if plan.sides:
            up = [(i, i + 1) for i in range(count - 1)]
            above = lax.ppermute(plane, "rows", up)
            below = lax.ppermute(plane, "rows", [(b, a) for a, b in up])
            if plan.sides == 2:
                plane = jnp.concatenate([above, plane, below], axis=1)
            else:
                plane = jnp.concatenate(
                    [jnp.where(r == 0, plane, above), jnp.where(r == 0, below, plane)], axis=1
                )
        plane = plane.reshape(slices, plan.stored, tiles // GROUP, GROUP, LANES)
        source = plane.transpose(0, 2, 3, 1, 4)
    if count <= 2:
        row_mats = [jnp.asarray(np.stack([plan.row_matrix(s, k) for k in range(count)])) for s in range(slices)]
    else:
        row_mats = [plan.row_matrix(s, r, jnp)[None] for s in range(slices)]
    vmem = pl.BlockSpec(memory_space=pltpu.VMEM)
    scratch = [
        pltpu.VMEM((2, tiles + 2, waves * plan.high[0], 2 * LANES), jnp.bfloat16),
        pltpu.VMEM((2, GROUP, waves * plan.high[0], 2 * LANES), jnp.bfloat16),
        pltpu.VMEM((waves, 2, tiles, LANES), jnp.float32),
        pltpu.VMEM((waves, 2, plan.high[0], LANES), jnp.float32),
    ]
    params = {}
    if gather:
        groups = across // GROUP
        scratch = [pltpu.VMEM((slices, groups, GROUP, plan.stored, LANES), jnp.bfloat16)] + scratch
        for size in (groups - 1, groups - 1, 3, 3, 4, 4):
            scratch.append(pltpu.SemaphoreType.DMA((slices, size)))
        scratch.append(pltpu.SemaphoreType.DMA((slices,)))
        params = dict(collective_id=0, has_side_effects=True)
    return pl.pallas_call(
        functools.partial(device_kernel, plan, waves, gather),
        out_shape=jax.ShapeDtypeStruct((2, waves, rows_local, width * across), jnp.bfloat16),
        in_specs=[pl.BlockSpec(memory_space=pltpu.SMEM)] + [vmem] * (2 + slices),
        out_specs=vmem,
        scratch_shapes=scratch,
        compiler_params=pltpu.CompilerParams(vmem_limit_bytes=60 * 1024 * 1024, **params),
    )(tilt_index, source, jnp.asarray(tile_band()), *row_mats)


def solution(mesh):
    placed = (P(None, "rows", "wave"), P("wave", None))
    return jax.shard_map(
        per_device,
        mesh=mesh,
        in_specs=placed,
        out_specs=P(None, "wave", "rows", None),
        check_vma=False,
    )
```

```python
import functools
import math

import jax
import jax.numpy as jnp
import numpy as np
from jax import lax
from jax.experimental import pallas as pl
from jax.experimental.pallas import tpu as pltpu
from jax.sharding import PartitionSpec as P

TAPS = 33
REACH = TAPS // 2
LANES = 128
GROUP = 4
MESH = pl.DeviceIdType.MESH

MIDDLE = 1.5
SIN_COEF = (9.99999997e-01, -1.66666606e-01, 8.33311822e-03, -1.98143924e-04, 2.61811836e-06)
COS_COEF = (9.99999970e-01, -4.99999341e-01, 4.16643157e-02, -1.38594940e-03, 2.32943501e-05)


def tap_parts(offset, np=np):
    centred = (offset - REACH).astype(np.float32)
    angle_val = np.float32(math.pi) * centred * centred / np.float32(TAPS)
    valid = (offset >= 0) & (offset < TAPS)
    weight = np.where(valid, 1.0 / math.sqrt(TAPS), 0.0).astype(np.float32)
    real_part = (np.cos(angle_val) * weight).astype(jnp.bfloat16)
    imag_part = (np.sin(angle_val) * weight).astype(jnp.bfloat16)
    return real_part, imag_part


def tile_band():
    inner = np.arange(LANES)[:, None]
    outer = np.arange(LANES)[None, :]
    beside = np.where(inner < LANES // 2, inner + LANES, inner - LANES)
    parts = []
    for source in (inner, beside):
        real_part, imag_part = tap_parts(source - outer + REACH)
        top = np.concatenate([real_part, imag_part], axis=1)
        low = np.concatenate([-imag_part, real_part], axis=1)
        parts.append(np.concatenate([top, low], axis=0))
    return np.concatenate(parts, axis=0)


class Plan:
    def __init__(self, slices, rows_local, count):
        self.sides = min(count - 1, 2)
        self.rows_local, self.count, self.slices = rows_local, count, slices
        self.high = [rows_local + self.sides * REACH * (slices - s) for s in range(slices + 1)]
        self.stored = rows_local * (1 + self.sides)

    def start(self, s, r):
        if self.sides == 0:
            return 0 * r
        if self.sides == 1:
            return r * (2 * self.rows_local - self.high[s])
        return r * self.rows_local - REACH * (self.slices - s)

    def stored_offset(self, s, r):
        if self.sides == 2:
            return self.rows_local - REACH * (self.slices - s)
        return self.start(s, r)

    def row_matrix(self, s, r, np=np):
        out_row = np.arange(self.high[s + 1])[:, None] + self.start(s + 1, r)
        in_row = np.arange(self.high[s])[None, :] + self.start(s, r)
        inside = (in_row >= 0) & (in_row < self.rows_local * self.count)
        real_part, imag_part = tap_parts(np.where(inside, in_row - out_row + REACH, -1), np)
        top = np.concatenate([real_part, -imag_part], axis=1)
        low = np.concatenate([imag_part, real_part], axis=1)
        return np.concatenate([top, low], axis=0)


def horner(square, coefs):
    total = square * coefs[-1] + coefs[-2]
    for coef in coefs[-3::-1]:
        total = total * square + coef
    return total


def transmission(pot):
    turn = 3.0 * pot.astype(jnp.float32) - MIDDLE
    square = turn * turn
    return horner(square, COS_COEF), horner(square, SIN_COEF) * turn


def modulo(value, size):
    if size & (size - 1) == 0:
        return value & (size - 1)
    return lax.rem(lax.rem(value, size) + size, size)


def gather_steps(plan, column_groups, shard, full, sems):
    send1, recv1, send2, recv2, send3, recv3, own = sems
    me, r = lax.axis_index("wave"), lax.axis_index("rows")
    z, q = me // GROUP, me % GROUP
    x, c = q // 2, q % 2
    rows = plan.rows_local
    flip_x = z * GROUP + (1 - x) * 2 + c
    sibling = z * GROUP + x * 2 + (1 - c)

    def block(s, column, row_dev, trimmed):
        need = REACH * (plan.slices - s) if trimmed else rows
        start = row_dev * rows + (1 - row_dev) * (rows - need)
        return full.at[s, :, column, pl.ds(pl.multiple_of(start, REACH), need), :]

    def remote(src, dst, send, recv, wave, row):
        return pltpu.make_async_remote_copy(
            src_ref=src, dst_ref=dst, send_sem=send, recv_sem=recv, device_id=(wave, row), device_id_type=MESH
        )

    barrier = pltpu.get_barrier_semaphore()
    others = [((z + d) % column_groups * GROUP + q, r) for d in range(1, column_groups)]
    peers = others + [(flip_x, r), (me, 1 - r), (sibling, r)]
    for peer in peers:
        pl.semaphore_signal(barrier, inc=1, device_id=peer, device_id_type=MESH)
    pl.semaphore_wait(barrier, len(peers))

    first, second, third, local = [], [], [], []
    for s in range(plan.slices):
        place = full.at[s, z, q, pl.ds(pl.multiple_of(r * rows, rows), rows), :]
        local.append(pltpu.make_async_copy(shard.at[s], place, own.at[s]))
        first.append([
            remote(shard.at[s], place, send1.at[s, d], recv1.at[s, d], *others[d])
            for d in range(column_groups - 1)
        ])
        mine, mine_cut = block(s, q, r, False), block(s, q, r, True)
        beyond_cut = block(s, (1 - x) * 2 + c, r, True)
        second.append([
            remote(mine, mine, send2.at[s, 0], recv2.at[s, 0], flip_x, r),
            remote(mine_cut, mine_cut, send2.at[s, 1], recv2.at[s, 1], me, 1 - r),
            remote(beyond_cut, beyond_cut, send2.at[s, 2], recv2.at[s, 2], me, 1 - r),
        ])
        beyond = (1 - x) * 2 + c
        held = [
            mine,
            block(s, beyond, r, False),
            block(s, q, 1 - r, True),
            block(s, beyond, 1 - r, True),
        ]
        third.append([
            remote(held[k], held[k], send3.at[s, k], recv3.at[s, k], sibling, r) for k in range(4)
        ])
    return local, first, second, third


def device_kernel(plan, waves, gather, tilt, shard, band_given, *rest):
    slices = plan.slices
    mats_given, out = rest[:slices], rest[slices]
    row_mats = rest[slices + 1 : 2 * slices + 1]
    band, sent, load_sems, out_sems = rest[2 * slices + 1 : 2 * slices + 5]
    scratch = rest[2 * slices + 5 :]
    r = lax.axis_index("rows")
    variant = r if plan.count <= 2 else 0
    loads = [pltpu.make_async_copy(band_given, band, load_sems.at[slices])]
    for s in range(slices):
        loads.append(pltpu.make_async_copy(mats_given[s].at[variant], row_mats[s], load_sems.at[s]))
    for copy in loads:
        copy.start()
    if gather:
        full, moved, halves, col_turn, row_turn = scratch[:5]
    else:
        full = shard
        moved, halves, col_turn, row_turn = scratch[:4]
    column_groups = full.shape[1]
    tiles = column_groups * GROUP
    plane_rows = plan.rows_local * plan.count

    if gather:
        local, first, second, third = gather_steps(plan, column_groups, shard, full, scratch[5:])
        for s in range(slices):
            for copy in first[s]:
                copy.start()
            local[s].start()

    def relay_columns(s):
        if gather:
            for copy in first[s]:
                copy.wait_recv()
            local[s].wait()
            second[s][0].start()
            second[s][1].start()
            third[s][0].start()

    def relay_across(s):
        if gather:
            second[s][0].wait_recv()
            second[s][2].start()
            third[s][1].start()

    def relay_rows(s):
        if gather:
            for k in (1, 2):
                second[s][k].wait_recv()
                third[s][k + 1].start()

    def arrive(s):
        if gather:
            for copy in third[s]:
                copy.wait_recv()

    for b in range(waves):
        column = lax.broadcasted_iota(jnp.int32, (tiles, LANES), 0) * LANES
        column = column + lax.broadcasted_iota(jnp.int32, (tiles, LANES), 1)
        size = tiles * LANES
        turn = modulo(tilt[b, 1] * column, size).astype(jnp.float32) * (2.0 * math.pi / size)
        col_turn[b, 0] = jnp.cos(turn)
        col_turn[b, 1] = jnp.sin(turn)
        row = lax.broadcasted_iota(jnp.int32, (plan.high[0], LANES), 0) + plan.start(0, r)
        turn = modulo(tilt[b, 0] * row, plane_rows).astype(jnp.float32) * (2.0 * math.pi / plane_rows)
        turn = turn + slices * MIDDLE
        row_turn[b, 0] = jnp.cos(turn)
        row_turn[b, 1] = jnp.sin(turn)
    for half in range(2):
        for edge in (0, tiles + 1):
            moved[half, edge] = jnp.zeros(moved.shape[2:], moved.dtype)

    def transmit(s, group, lane, source):
        high = plan.high[s]
        offset = plan.stored_offset(s, r)
        for k in range(high // REACH):
            at = offset + k * REACH
            if not isinstance(at, int):
                at = pl.multiple_of(at, REACH)
            t_re, t_im = transmission(full[s, group, lane, pl.ds(at, REACH), :])
            for b in range(waves):
                w_re, w_im = source(k, b)
                to = moved.at[s % 2, group * GROUP + lane + 1, pl.ds(b * high + k * REACH, REACH)]
                to[:, :LANES] = (w_re * t_re - w_im * t_im).astype(jnp.bfloat16)
                to[:, LANES:] = (w_re * t_im + w_im * t_re).astype(jnp.bfloat16)

    relay_columns(0)
    relay_columns(1)
    relay_across(0)
    relay_columns(2)
    relay_columns(3)
    relay_across(1)
    relay_rows(0)
    arrive(0)

    def begin(group, carry):
        for lane in range(GROUP):
            tile = group * GROUP + lane

            def source(k, b):
                c_re, c_im = col_turn[b, 0, pl.ds(tile, 1), :], col_turn[b, 1, pl.ds(tile, 1), :]
                span = pl.ds(k * REACH, REACH)
                r_re, r_im = row_turn[b, 0, span, :], row_turn[b, 1, span, :]
                return r_re * c_re - r_im * c_im, r_re * c_im + r_im * c_re

            transmit(0, group, lane, source)
        return carry

    half = column_groups // 2
    lax.fori_loop(0, half, begin, 0)
    relay_across(2)
    relay_rows(1)
    lax.fori_loop(half, column_groups, begin, 0)

    def column_pass(s, group):
        rows = waves * plan.high[s]
        tile = group * GROUP

        def tiles_from(first_tile):
            return moved[s % 2, pl.ds(first_tile, GROUP), pl.ds(0, rows)].reshape(GROUP * rows, 2 * LANES)

        lane = lax.broadcasted_iota(jnp.int32, (GROUP * rows, 2 * LANES), 1) % LANES
        beside = jnp.where(lane < LANES // 2, tiles_from(tile + 2), tiles_from(tile))
        window = jnp.concatenate([tiles_from(tile + 1), beside], axis=1)
        half_step = jnp.dot(window, band[...], preferred_element_type=jnp.float32).astype(jnp.bfloat16)
        halves[group % 2, :, pl.ds(0, rows)] = half_step.reshape(GROUP, rows, 2 * LANES)

    def store_of(group):
        start = group * GROUP * LANES
        start = start if isinstance(start, int) else pl.multiple_of(start, LANES)
        place = out.at[:, :, :, pl.ds(start, GROUP * LANES)]
        return pltpu.make_async_copy(sent.at[group], place, out_sems.at[group])

    def row_pass(s, group):
        high, low = plan.high[s], plan.high[s + 1]
        matrix = row_mats[s][...]
        for lane in range(GROUP):
            stacked = jnp.concatenate(
                [
                    jnp.concatenate(
                        [
                            halves[group % 2, lane, pl.ds(b * high, high), pl.ds(p * LANES, LANES)]
                            for b in range(waves)
                        ],
                        axis=1,
                    )
                    for p in range(2)
                ],
                axis=0,
            )
            result = jnp.dot(matrix, stacked, preferred_element_type=jnp.float32)
            if s + 1 < slices:

                def source(k, b):
                    span_b = slice(b * LANES, (b + 1) * LANES)
                    at = k * REACH
                    return result[at : at + REACH, span_b], result[low + at : low + at + REACH, span_b]

                transmit(s + 1, group, lane, source)
            else:
                columns = pl.ds(lane * LANES, LANES)
                for p in range(2):
                    for b in range(waves):
                        part = result[p * low : (p + 1) * low, b * LANES : (b + 1) * LANES]
                        sent[group, p, b, :, columns] = part.astype(jnp.bfloat16)
        if s + 1 == slices:
            store_of(group).start()

    last = column_groups - 1
    for copy in loads:
        copy.wait()
    column_pass(0, 0)
    relay_across(3)
    arrive(1)
    for s in range(slices):

        def advance(group, carry):
            column_pass(s, group + 1)
            row_pass(s, group)
            return carry

        if s + 2 < slices:
            lax.fori_loop(0, half, advance, 0)
            relay_rows(s + 2)
            lax.fori_loop(half, last, advance, 0)
        else:
            lax.fori_loop(0, last, advance, 0)
        row_pass(s, last)
        if s + 1 < slices:
            column_pass(s + 1, 0)
        if s + 2 < slices:
            arrive(s + 2)

    for group in range(column_groups):
        store_of(group).wait()
    if gather:
        for s in range(slices):
            for copy in first[s] + second[s] + third[s]:
                copy.wait_send()


def per_device(potential, tilt_index):
    slices, rows_local, width = potential.shape
    waves = tilt_index.shape[0]
    across, count = lax.axis_size("wave"), lax.axis_size("rows")
    plan = Plan(slices, rows_local, count)
    r = lax.axis_index("rows")
    tiles = width * across // LANES
    gather = count == 2 and width == LANES and across % GROUP == 0
    source = potential
    if not gather:
        plane = lax.all_gather(potential, "wave", axis=2, tiled=True)
        if plan.sides:
            up = [(i, i + 1) for i in range(count - 1)]
            above = lax.ppermute(plane, "rows", up)
            below = lax.ppermute(plane, "rows", [(b, a) for a, b in up])
            if plan.sides == 2:
                plane = jnp.concatenate([above, plane, below], axis=1)
            else:
                plane = jnp.concatenate(
                    [jnp.where(r == 0, plane, above), jnp.where(r == 0, below, plane)], axis=1
                )
        plane = plane.reshape(slices, plan.stored, tiles // GROUP, GROUP, LANES)
        source = plane.transpose(0, 2, 3, 1, 4)
    if count <= 2:
        row_mats = [jnp.asarray(np.stack([plan.row_matrix(s, k) for k in range(count)])) for s in range(slices)]
    else:
        row_mats = [plan.row_matrix(s, r, jnp)[None] for s in range(slices)]
    vmem = pl.BlockSpec(memory_space=pltpu.VMEM)
    anywhere = pl.BlockSpec(memory_space=pl.ANY)
    high = plan.high
    always = [pltpu.VMEM((2 * high[s + 1], 2 * high[s]), jnp.bfloat16) for s in range(slices)]
    always += [
        pltpu.VMEM((4 * LANES, 2 * LANES), jnp.bfloat16),
        pltpu.VMEM((tiles // GROUP, 2, waves, rows_local, GROUP * LANES), jnp.bfloat16),
        pltpu.SemaphoreType.DMA((slices + 1,)),
        pltpu.SemaphoreType.DMA((tiles // GROUP,)),
    ]
    scratch = [
        pltpu.VMEM((2, tiles + 2, waves * plan.high[0], 2 * LANES), jnp.bfloat16),
        pltpu.VMEM((2, GROUP, waves * plan.high[0], 2 * LANES), jnp.bfloat16),
        pltpu.VMEM((waves, 2, tiles, LANES), jnp.float32),
        pltpu.VMEM((waves, 2, plan.high[0], LANES), jnp.float32),
    ]
    params = {}
    if gather:
        groups = across // GROUP
        scratch = [pltpu.VMEM((slices, groups, GROUP, plan.stored, LANES), jnp.bfloat16)] + scratch
        for size in (groups - 1, groups - 1, 3, 3, 4, 4):
            scratch.append(pltpu.SemaphoreType.DMA((slices, size)))
        scratch.append(pltpu.SemaphoreType.DMA((slices,)))
        params = dict(collective_id=0, has_side_effects=True)
    return pl.pallas_call(
        functools.partial(device_kernel, plan, waves, gather),
        out_shape=jax.ShapeDtypeStruct((2, waves, rows_local, width * across), jnp.bfloat16),
        in_specs=[pl.BlockSpec(memory_space=pltpu.SMEM), vmem] + [anywhere] * (1 + slices),
        out_specs=anywhere,
        scratch_shapes=always + scratch,
        compiler_params=pltpu.CompilerParams(vmem_limit_bytes=60 * 1024 * 1024, **params),
    )(tilt_index, source, jnp.asarray(tile_band()), *row_mats)


def solution(mesh):
    placed = (P(None, "rows", "wave"), P("wave", None))
    return jax.shard_map(
        per_device,
        mesh=mesh,
        in_specs=placed,
        out_specs=P(None, "wave", "rows", None),
        check_vma=False,
    )
```
